32 devices in a mesh: grp: 1, frame: 32 (over z, y, x, core).
Axes of the slice: x: 2, y: 2, z: 4, core: 2. Of those that a mesh axis runs over, the one named last changes fastest.
Arguments:
- tokens: bfloat16 [8192, 2240], P(('grp', 'frame')), may hold values from -16 to 16
- w_query: bfloat16 [1792, 2240], P('frame'), may hold values from -0.125 to 0.125
- w_keyval: bfloat16 [3584, 2240], P('frame'), may hold values from -0.125 to 0.125
- taps: float32 [3, 1792], replicated, may hold values from -1 to 1
Outputs:
- mixed: bfloat16 [8192, 1792], P(('grp', 'frame'))
The draws below stay inside these ranges and needn't reach their ends.
All inputs are finite; a program needn't handle non-finite values.
Results may differ from the reference program's by a relative error of at most 0.0051.
Values may be sent and summed in bfloat16 or wider, within the bound.
A program may use at most 128 MiB of HBM per device.

```python
import jax
import jax.numpy as jnp
from jax import lax

D = 2240
HEADS = 16
HDIM = 112
HEIGHT = 32
WIDTH = 32
TOK_DEV = 256
FRAMES = 8
TOKENS = 8192
CH = 1792


def draw_tokens(key, part):
    key_noise, key_level, key_offset = jax.random.split(key, 3)
    blocks = TOKENS // TOK_DEV
    rising = 3.0 ** (jnp.arange(blocks, dtype=jnp.float32) / max(blocks - 1, 1))
    level = jax.random.uniform(key_level, (blocks, 1), jnp.float32, 0.7, 1.4) * rising[:, None]
    offsets = jax.random.normal(key_offset, (blocks, D), jnp.float32) * level
    noise = jax.random.normal(key_noise, (TOKENS, D), jnp.float32)
    values = noise + jnp.repeat(offsets, TOK_DEV, axis=0)
    return jnp.clip(values, -16.0, 16.0).astype(jnp.bfloat16)


def levels(rng, shape, cuts, smallest, high):
    gain = 1.0
    for axis_at, shards_of in cuts:
        heights = jax.random.uniform(jax.random.fold_in(jax.random.fold_in(rng, 6), axis_at), (shards_of,), jnp.float32, smallest / len(cuts), high / len(cuts))
        gain = gain * jnp.repeat(jnp.exp(heights), shape[axis_at] // shards_of).reshape((-1,) + (1,) * (len(shape) - 1 - axis_at))
    return gain


def scatter_about(own_key, dims, spread, bound, pieces=(), held_as=jnp.bfloat16):
    values = jax.random.normal(own_key, dims, jnp.float32) * spread
    if len(pieces) > 0:
        values = levels(own_key, dims, pieces, -0.22, 0.18) * values
    return jnp.clip(values, min=-bound, max=bound).astype(held_as)


def setup_inputs(seed: int = 0, part: int = 0) -> dict:
    keys = jax.random.split(jax.random.key(seed), 5)
    part_keys = jax.random.split(jax.random.fold_in(keys[4], part), 5)
    return {
        "tokens": draw_tokens(jax.random.fold_in(jax.random.fold_in(keys[4], part), 71), part),
        "w_query": scatter_about(keys[1], (CH, D), D ** -0.5, 0.125, ((0, 32),)),
        "w_keyval": scatter_about(keys[2], (2 * CH, D), D ** -0.5, 0.125, ((0, 32),)),
        "taps": jnp.clip(jax.random.uniform(keys[3], (3, CH), jnp.float32, -1.0, 1.0), -1.0, 1.0),
    }


epsilon = 1e-06

def normalize(rows_in):
    values = rows_in.astype(jnp.float32)
    scale_inv = lax.rsqrt(lax.optimization_barrier(jnp.mean(values * values, axis=-1, keepdims=True)) + epsilon)
    return (values * scale_inv).astype(jnp.bfloat16)

def temporal_mix(by_frame, taps):
    zeros_row = jnp.zeros_like(by_frame[:1])
    earlier = jnp.concatenate([zeros_row, by_frame[:-1]], 0)
    later_frame = jnp.concatenate([by_frame[1:], zeros_row], 0)
    return taps[0] * earlier + taps[1] * by_frame + taps[2] * later_frame

def reference(tokens, w_query, w_keyval, taps):
    channels = HEADS * HDIM
    blocks = TOKENS // TOK_DEV

    def project(block_rows):
        normed = normalize(block_rows)
        query_lin = jnp.dot(normed, w_query.T, preferred_element_type=jnp.float32)
        keyval_lin = jnp.dot(normed, w_keyval.T, preferred_element_type=jnp.float32)
        query_feats = jax.nn.relu(query_lin).astype(jnp.bfloat16)
        key_feats = jax.nn.relu(keyval_lin[:, :channels]).astype(jnp.bfloat16)
        value_proj = keyval_lin[:, channels:].astype(jnp.bfloat16)
        key_heads = key_feats.astype(jnp.float32).reshape(-1, HEADS, HDIM)
        value_heads = value_proj.astype(jnp.float32).reshape(-1, HEADS, HDIM)
        state = jnp.einsum('thd,the->hde', key_heads, value_heads, precision=lax.Precision.HIGHEST)
        return (query_feats, state, lax.optimization_barrier(jnp.sum(key_heads, axis=0)))
    query_feats, states, key_sums = lax.map(project, tokens.reshape(blocks, TOK_DEV, D))
    state = lax.optimization_barrier(jnp.sum(states, axis=0))
    key_total = lax.optimization_barrier(jnp.sum(key_sums, axis=0))
    query_heads = query_feats.reshape(TOKENS, HEADS, HDIM).astype(jnp.float32)
    numer = jnp.einsum('thd,hde->the', query_heads, state, precision=lax.Precision.HIGHEST)
    denom = jnp.einsum('thd,hd->th', query_heads, key_total, precision=lax.Precision.HIGHEST) + epsilon
    attended = (numer / denom[:, :, None]).reshape(TOKENS, channels).astype(jnp.bfloat16)
    by_frame = attended.reshape(FRAMES, HEIGHT * WIDTH, channels).astype(jnp.float32)
    return temporal_mix(by_frame, taps).reshape(TOKENS, channels).astype(jnp.bfloat16)
```

```python
import jax
import jax.numpy as jnp
from jax import lax
from jax.experimental import pallas as pl
from jax.experimental.pallas import tpu as pltpu
from jax.sharding import PartitionSpec as P

HEADS = 16
HDIM = 112
HEIGHT = 32
WIDTH = 32


epsilon = 1e-06


def from_behind(value, axis, steps):
    count = lax.axis_size(axis)
    leading, last = (max(0, -steps), min(count, count - steps))
    return lax.ppermute(value, axis, [(source, source + steps) for source in range(leading, last)])


def normalize(rows_in):
    values = rows_in.astype(jnp.float32)
    scale_inv = lax.rsqrt(jnp.mean(values * values, axis=-1, keepdims=True) + epsilon)
    return (values * scale_inv).astype(jnp.bfloat16)


def local(tokens, w_query, w_keyval, taps):
    channels = HEADS * HDIM
    rows_here = tokens.shape[0]
    normed = normalize(tokens)

    def project_rows(weight_rows):
        return lax.dot_general(
            normed, weight_rows, (((1,), (1,)), ((), ())), preferred_element_type=jnp.float32
        )

    keyval_lin = project_rows(lax.all_gather(w_keyval, "frame", axis=0, tiled=True))
    key_feats = jax.nn.relu(keyval_lin[:, :channels]).astype(jnp.bfloat16)
    value_proj = keyval_lin[:, channels:].astype(jnp.bfloat16)
    key_heads = key_feats.reshape(rows_here, HEADS, HDIM)
    value_heads = value_proj.reshape(rows_here, HEADS, HDIM)
    local_state = jnp.einsum(
        "thd,the->hde", key_heads, value_heads, preferred_element_type=jnp.float32
    )
    local_keys = jnp.sum(key_heads.astype(jnp.float32), axis=0)
    query_lin = project_rows(lax.all_gather(w_query, "frame", axis=0, tiled=True))
    query_feats = jax.nn.relu(query_lin).astype(jnp.bfloat16)
    state, key_total = lax.psum((local_state, local_keys), "frame")
    query_heads = query_feats.reshape(rows_here, HEADS, HDIM).astype(jnp.float32)
    numer = jnp.einsum("thd,hde->the", query_heads, state, precision=lax.Precision.HIGHEST)
    denom = (
        jnp.einsum("thd,hd->th", query_heads, key_total, precision=lax.Precision.HIGHEST) + epsilon
    )
    attended = (numer / denom[:, :, None]).reshape(rows_here, channels).astype(jnp.bfloat16)
    strips = HEIGHT * WIDTH // rows_here
    earlier = from_behind(attended, "frame", strips)
    later_frame = from_behind(attended, "frame", -strips)
    mixed = (
        taps[0] * earlier.astype(jnp.float32)
        + taps[1] * attended.astype(jnp.float32)
        + taps[2] * later_frame.astype(jnp.float32)
    ).astype(jnp.bfloat16)
    return mixed


COLUMNS = 4
CORES = 2
LAYER = COLUMNS * CORES
LOWEST = -3.0e38
NT = (((1,), (1,)), ((), ()))


def fused_kernel(depth, tok_ref, wq_ref, wkv_ref, taps_ref, out_ref,
                 tokbuf, nbuf, wqb, wkvb, feats, st, sib_in, st_out, st_in, st_sum, full,
                 att, halo, mixbuf,
                 local_sem, move_send, wrecv, zsend, sibsend, trecv, tsend, tfsend,
                 s1_send, s1_recv, s2_send, s2_recv, s3_send, s3_recv,
                 hsend, hrecv, osend, orecv):
    me = lax.axis_index("frame")
    z = me // LAYER
    inner = me % LAYER
    col = inner // CORES
    core = inner % CORES
    other = 1 - core
    yy = col // 2
    xx = col % 2

    def dev(layer, column, which):
        return {"frame": layer * LAYER + column * CORES + which}

    def near(o):
        return 2 * ((yy + o // 2) % 2) + (xx + o % 2) % 2

    sib = dev(z, col, other)

    def rcopy(src, dst, ssem, rsem, to):
        return pltpu.make_async_remote_copy(
            src_ref=src, dst_ref=dst, send_sem=ssem, recv_sem=rsem,
            device_id=to, device_id_type=pl.DeviceIdType.MESH)

    barrier = pltpu.get_barrier_semaphore()
    for step in range(1, LAYER):
        pl.semaphore_signal(barrier, inc=1, device_id={"frame": z * LAYER + (inner + step) % LAYER},
                            device_id_type=pl.DeviceIdType.MESH)
    for step in range(1, depth):
        for which in range(CORES):
            pl.semaphore_signal(barrier, inc=1, device_id=dev((z + step) % depth, col, which),
                                device_id_type=pl.DeviceIdType.MESH)
    pl.semaphore_wait(barrier, LAYER - 1 + (depth - 1) * CORES)

    to_col = inner % COLUMNS
    to_core = inner // COLUMNS
    keep = jnp.logical_and(to_col == col, to_core == core)

    def move():
        return rcopy(wkv_ref, wkvb.at[z, to_core], move_send.at[0], wrecv.at[z, 1, to_core], dev(z, to_col, to_core))

    kv_local = pltpu.make_async_copy(wkv_ref, wkvb.at[z, core], local_sem.at[1])
    q_local = pltpu.make_async_copy(wq_ref, wqb.at[z, core], local_sem.at[0])

    @pl.when(jnp.logical_not(keep))
    def _():
        move().start()

    @pl.when(keep)
    def _():
        kv_local.start()

    q_local.start()

    def wslot(t, part, c):
        return (wqb, wkvb)[part].at[t, c]

    def zcopy(t, part, way):
        src = wslot(t, part, core)
        return rcopy(src, src, zsend.at[(way + 1) // 2, t, part], wrecv.at[t, part, core], dev(z + way, col, core))

    def sibcopy(t, part):
        src = wslot(t, part, core)
        return rcopy(src, src, sibsend.at[t, part], wrecv.at[t, part, core], sib)

    def sends_of(t, part, way, act):
        @pl.when(jnp.logical_and(z + way >= 0, z + way < depth))
        def _():
            act(zcopy(t, part, way))

    def begin(c):
        c.start()

    def pass_on(k, part):
        for way in (1, -1):
            t = z - way * k

            @pl.when(jnp.logical_and(t >= 0, t < depth))
            def _():
                sibcopy(t, part).wait_recv()
                sends_of(t, part, way, begin)
                sibcopy(t, part).start()

    side = (None, dev(z, near(1), core), dev(z, near(2), core))

    def tcopy(o, h):
        return rcopy(tok_ref.at[h], tokbuf.at[col, h], tsend.at[o - 1, h], trecv.at[col, h], side[o])

    def tforward(o):
        b, h = near(o), o - 1
        return rcopy(tokbuf.at[b, h], tokbuf.at[b, h], tfsend.at[o - 1], trecv.at[b, h], side[3 - o])

    def twait(o, h):
        b = near(o)
        rcopy(tokbuf.at[b, h], tokbuf.at[b, h], tfsend.at[0], trecv.at[b, h], side[1]).wait_recv()

    q_local.wait()
    sends_of(z, 0, 1, begin)
    sends_of(z, 0, -1, begin)
    sibcopy(z, 0).start()
    tcopy(1, 0).start()
    tcopy(2, 1).start()
    tcopy(1, 1).start()
    tcopy(2, 0).start()

    def norm_into(b, h, rows):
        values = rows.astype(jnp.float32)
        scale_inv = lax.rsqrt(jnp.mean(values * values, axis=-1, keepdims=True) + epsilon)
        nbuf[b, h] = (values * scale_inv).astype(jnp.bfloat16)

    for h in range(2):
        norm_into(col, h, tok_ref[h])

    @pl.when(keep)
    def _():
        kv_local.wait()

    @pl.when(jnp.logical_not(keep))
    def _():
        rcopy(wkv_ref, wkvb.at[z, core], move_send.at[0], wrecv.at[z, 1, core], sib).wait_recv()

    sends_of(z, 1, 1, begin)
    sends_of(z, 1, -1, begin)
    sibcopy(z, 1).start()

    def sib_wait(k):
        for way in ((1, -1) if k else (1,)):
            t = z - way * k

            @pl.when(jnp.logical_and(t >= 0, t < depth))
            def _():
                for part in range(2):
                    slot = wslot(t, part, other)
                    rcopy(slot, slot, sibsend.at[t, part], wrecv.at[t, part, other], sib).wait_recv()

    def project(t, o):
        b = near(o)
        toks = nbuf[b].reshape(nbuf.shape[1] * nbuf.shape[2], nbuf.shape[3])
        parts = [lax.dot_general(wqb[t, c], toks, NT, preferred_element_type=jnp.float32) for c in range(2)]
        kv = wkvb[t].reshape(2 * wkvb.shape[2], wkvb.shape[3])
        lin = lax.dot_general(kv, toks, NT, preferred_element_type=jnp.float32)
        query = jnp.concatenate(parts, axis=0)
        floor = jnp.where(t < depth // 2, 0.0, LOWEST)
        feats[t, b, 0] = jnp.maximum(query, 0.0).astype(jnp.bfloat16)
        lin = jnp.maximum(lin, floor).astype(jnp.bfloat16)
        feats[t, b, 1] = lin[:HDIM]
        feats[t, b, 2] = lin[HDIM:]

    def compute(count, offset_of, o_from, o_count):
        def body(i, carry):
            t = z + offset_of(i // o_count)

            @pl.when(jnp.logical_and(t >= 0, t < depth))
            def _():
                project(t, o_from + i % o_count)
            return carry
        lax.fori_loop(0, count * o_count, body, 0)

    def norm_recv(o):
        b = near(o)
        for h in range(2):
            norm_into(b, h, tokbuf[b, h])

    pass_on(1, 0)
    sib_wait(0)
    compute(1, lambda i: 0, 0, 1)
    twait(1, 0)
    tforward(1).start()
    twait(2, 1)
    tforward(2).start()
    pass_on(1, 1)
    sib_wait(1)
    compute(2, lambda i: 2 * i - 1, 0, 1)
    pass_on(2, 0)
    twait(1, 1)
    norm_recv(1)
    twait(2, 0)
    norm_recv(2)
    compute(3, lambda i: i - 1, 1, 2)
    pass_on(2, 1)
    sib_wait(2)
    compute(2, lambda i: 4 * i - 2, 0, 3)
    pass_on(3, 0)
    twait(3, 0)
    twait(3, 1)
    norm_recv(3)
    compute(5, lambda i: i - 2, 3, 1)
    pass_on(3, 1)
    sib_wait(3)
    compute(2, lambda i: 6 * i - 3, 0, 4)

    half = depth // 2
    ones = jnp.ones((st.shape[1] - HDIM, feats.shape[4]), jnp.bfloat16)
    for t in range(depth):
        total = None
        for b in range(COLUMNS):
            values = jnp.concatenate([feats[half + t // 2, b, 1 + t % 2], ones], axis=0)
            term = lax.dot_general(values, feats[t // 2, b, 1 + t % 2], NT, preferred_element_type=jnp.float32)
            total = term if total is None else total + term
        st[t] = total
    first = rcopy(st.at[pl.ds(2 * other, 2)], sib_in, s1_send.at[0], s1_recv.at[0], sib)
    first.start()
    first.wait()
    mine = (st[pl.ds(2 * core, 2)] + sib_in[...]).astype(jnp.bfloat16)
    st_out[...] = mine
    st_in[z] = mine

    def across(step):
        return rcopy(st_out, st_in.at[z], s2_send.at[step], s2_recv.at[z], dev((z + step) % depth, col, core))

    for step in range(1, depth):
        across(step).start()
    for step in range(1, depth):
        came = (z + step) % depth
        rcopy(st_out, st_in.at[came], s2_send.at[step], s2_recv.at[came], sib).wait_recv()
    total = st_in[0].astype(jnp.float32)
    for t in range(1, depth):
        total = total + st_in[t].astype(jnp.float32)
    st_sum[...] = total
    full[pl.ds(2 * core, 2)] = total
    third = rcopy(st_sum, full.at[pl.ds(2 * core, 2)], s3_send.at[0], s3_recv.at[0], sib)
    third.start()
    rcopy(st_sum, full.at[pl.ds(2 * other, 2)], s3_send.at[0], s3_recv.at[0], sib).wait_recv()

    def hcopy(way, t):
        d = (way + 1) // 2
        return rcopy(att.at[t, pl.ds(2 * d, 2)], halo.at[d, t], hsend.at[d, t], hrecv.at[d, t], dev(z + way, col, core))

    for way in (1, -1):
        @pl.when(jnp.logical_or(z - way < 0, z - way >= depth))
        def _():
            halo[(way + 1) // 2] = jnp.zeros(halo.shape[1:], halo.dtype)

    for t in range(depth):
        whole = full[t]
        high = whole.astype(jnp.bfloat16)
        low = (whole - high.astype(jnp.float32)).astype(jnp.bfloat16)
        for b in range(COLUMNS):
            query = feats[t, b, 0]
            both = (jnp.dot(high, query, preferred_element_type=jnp.float32)
                    + jnp.dot(low, query, preferred_element_type=jnp.float32))
            att[t, b] = (both[:HDIM] / (both[HDIM:HDIM + 1] + epsilon)).astype(jnp.bfloat16)
        for way in (1, -1):
            @pl.when(jnp.logical_and(z + way >= 0, z + way < depth))
            def _():
                hcopy(way, t).start()

    def ocopy(t, o):
        b = near(o)
        return rcopy(mixbuf.at[t, b], out_ref.at[t, col], osend.at[t, o], orecv.at[t, col], dev(z, b, core))

    for t in range(depth):
        for way in (1, -1):
            @pl.when(jnp.logical_and(z - way >= 0, z - way < depth))
            def _():
                hcopy(way, t).wait_recv()
        for x in range(2):
            even = att[t, x].astype(jnp.float32)
            odd = att[t, 2 + x].astype(jnp.float32)
            before = halo[1, t, x].astype(jnp.float32)
            after = halo[0, t, x].astype(jnp.float32)
            w = [taps_ref[k, t] for k in range(3)]
            mixbuf[t, x] = (w[0] * before + w[1] * even + w[2] * odd).astype(jnp.bfloat16)
            mixbuf[t, 2 + x] = (w[0] * even + w[1] * odd + w[2] * after).astype(jnp.bfloat16)
        for o in range(1, COLUMNS):
            ocopy(t, o).start()
        out_ref[t, col] = mixbuf[t, col]

    for t in range(depth):
        for o in range(1, COLUMNS):
            b = near(o)
            rcopy(mixbuf.at[t, b], out_ref.at[t, b], osend.at[t, o], orecv.at[t, b], dev(z, b, core)).wait_recv()
            ocopy(t, o).wait_send()
        for way in (1, -1):
            @pl.when(jnp.logical_and(z + way >= 0, z + way < depth))
            def _():
                hcopy(way, t).wait_send()
    third.wait_send()
    for step in range(1, depth):
        across(step).wait_send()

    @pl.when(jnp.logical_not(keep))
    def _():
        move().wait_send()

    for o in (1, 2):
        for h in range(2):
            tcopy(o, h).wait_send()
        tforward(o).wait_send()
    for t in range(depth):
        for part in range(2):
            sibcopy(t, part).wait_send()
            for way in (1, -1):
                @pl.when(way * (z - t) >= 0)
                def _():
                    sends_of(t, part, way, lambda c: c.wait_send())


def fused(tokens, w_query, w_keyval, taps):
    rows, width = tokens.shape
    depth = lax.axis_size("frame") // LAYER
    bf16, f32 = jnp.bfloat16, jnp.float32
    col = lax.axis_index("frame") % LAYER // CORES
    by_head = taps.reshape(taps.shape[0], HEADS // COLUMNS, COLUMNS, HDIM)
    own_taps = lax.dynamic_index_in_dim(by_head, col, 2, keepdims=False)[..., None]
    own_taps = jnp.broadcast_to(own_taps, own_taps.shape[:-1] + (rows,))
    dma = lambda *s: pltpu.SemaphoreType.DMA(s)
    ext = HDIM + 16
    vmem = pl.BlockSpec(memory_space=pltpu.VMEM)
    out = pl.pallas_call(
        lambda *refs: fused_kernel(depth, *refs),
        out_shape=jax.ShapeDtypeStruct((depth, COLUMNS, HDIM, rows), bf16),
        in_specs=[vmem] * 4,
        out_specs=vmem,
        scratch_shapes=[
            pltpu.VMEM((COLUMNS, 2, rows // 2, width), bf16),
            pltpu.VMEM((COLUMNS, 2, rows // 2, width), bf16),
            pltpu.VMEM((depth, 2, w_query.shape[0], width), bf16),
            pltpu.VMEM((depth, 2, w_keyval.shape[0], width), bf16),
            pltpu.VMEM((depth, COLUMNS, 3, HDIM, rows), bf16),
            pltpu.VMEM((depth, ext, HDIM), f32),
            pltpu.VMEM((2, ext, HDIM), f32),
            pltpu.VMEM((2, ext, HDIM), bf16),
            pltpu.VMEM((depth, 2, ext, HDIM), bf16),
            pltpu.VMEM((2, ext, HDIM), f32),
            pltpu.VMEM((depth, ext, HDIM), f32),
            pltpu.VMEM((depth, COLUMNS, HDIM, rows), bf16),
            pltpu.VMEM((2, depth, 2, HDIM, rows), bf16),
            pltpu.VMEM((depth, COLUMNS, HDIM, rows), bf16),
            dma(2), dma(1), dma(depth, 2, 2), dma(2, depth, 2), dma(depth, 2),
            dma(COLUMNS, 2), dma(2, 2), dma(2),
            dma(1), dma(1), dma(depth), dma(depth), dma(1), dma(1),
            dma(2, depth), dma(2, depth), dma(depth, COLUMNS), dma(depth, COLUMNS),
        ],
        compiler_params=pltpu.CompilerParams(collective_id=0, has_side_effects=True, vmem_limit_bytes=60000 * 1024),
    )(tokens.reshape(2, rows // 2, width), w_query, w_keyval, own_taps)
    return out.reshape(HEADS * HDIM, rows).T


def fits(count, tokens, w_query, w_keyval):
    return (
        w_keyval.shape[0] // count == HDIM
        and 2 * w_query.shape[0] // count == HDIM
        and count % LAYER == 0
        and count // LAYER * COLUMNS == HEADS
        and HEIGHT * WIDTH // (tokens.shape[0] // count) == COLUMNS
    )


def solution(mesh):
    placed = (P(("grp", "frame"), None), P("frame", None), P("frame", None), P())

    def step(tokens, w_query, w_keyval, taps):
        groups, count = mesh.shape["grp"], mesh.shape["frame"]
        part = jax.ShapeDtypeStruct((tokens.shape[0] // groups,) + tokens.shape[1:], tokens.dtype)
        body = fused if fits(count, part, w_query, w_keyval) else local
        return jax.shard_map(
            body, mesh=mesh, in_specs=placed, out_specs=P(("grp", "frame"), None), check_vma=False
        )(tokens, w_query, w_keyval, taps)

    return step
```

```python
import jax
import jax.numpy as jnp
from jax import lax
from jax.experimental import pallas as pl
from jax.experimental.pallas import tpu as pltpu
from jax.sharding import PartitionSpec as P

HEADS = 16
HDIM = 112
HEIGHT = 32
WIDTH = 32


epsilon = 1e-06


def from_behind(value, axis, steps):
    count = lax.axis_size(axis)
    leading, last = (max(0, -steps), min(count, count - steps))
    return lax.ppermute(value, axis, [(source, source + steps) for source in range(leading, last)])


def normalize(rows_in):
    values = rows_in.astype(jnp.float32)
    scale_inv = lax.rsqrt(jnp.mean(values * values, axis=-1, keepdims=True) + epsilon)
    return (values * scale_inv).astype(jnp.bfloat16)


def local(tokens, w_query, w_keyval, taps):
    channels = HEADS * HDIM
    rows_here = tokens.shape[0]
    normed = normalize(tokens)

    def project_rows(weight_rows):
        return lax.dot_general(
            normed, weight_rows, (((1,), (1,)), ((), ())), preferred_element_type=jnp.float32
        )

    keyval_lin = project_rows(lax.all_gather(w_keyval, "frame", axis=0, tiled=True))
    key_feats = jax.nn.relu(keyval_lin[:, :channels]).astype(jnp.bfloat16)
    value_proj = keyval_lin[:, channels:].astype(jnp.bfloat16)
    key_heads = key_feats.reshape(rows_here, HEADS, HDIM)
    value_heads = value_proj.reshape(rows_here, HEADS, HDIM)
    local_state = jnp.einsum(
        "thd,the->hde", key_heads, value_heads, preferred_element_type=jnp.float32
    )
    local_keys = jnp.sum(key_heads.astype(jnp.float32), axis=0)
    query_lin = project_rows(lax.all_gather(w_query, "frame", axis=0, tiled=True))
    query_feats = jax.nn.relu(query_lin).astype(jnp.bfloat16)
    state, key_total = lax.psum((local_state, local_keys), "frame")
    query_heads = query_feats.reshape(rows_here, HEADS, HDIM).astype(jnp.float32)
    numer = jnp.einsum("thd,hde->the", query_heads, state, precision=lax.Precision.HIGHEST)
    denom = (
        jnp.einsum("thd,hd->th", query_heads, key_total, precision=lax.Precision.HIGHEST) + epsilon
    )
    attended = (numer / denom[:, :, None]).reshape(rows_here, channels).astype(jnp.bfloat16)
    strips = HEIGHT * WIDTH // rows_here
    earlier = from_behind(attended, "frame", strips)
    later_frame = from_behind(attended, "frame", -strips)
    mixed = (
        taps[0] * earlier.astype(jnp.float32)
        + taps[1] * attended.astype(jnp.float32)
        + taps[2] * later_frame.astype(jnp.float32)
    ).astype(jnp.bfloat16)
    return mixed


COLUMNS = 4
CORES = 2
LAYER = COLUMNS * CORES
LOWEST = -3.0e38
NT = (((1,), (1,)), ((), ()))


def fused_kernel(depth, tok_ref, wq_ref, wkv_ref, taps_ref, out_ref,
                 tokbuf, nbuf, wqb, wkvb, feats, st, sib_in, st_out, st_in, st_sum, full,
                 att, halo, mixbuf,
                 local_sem, move_send, wrecv, zsend, sibsend, trecv, tsend, tfsend,
                 s1_send, s1_recv, s2_send, s2_recv, s3_send, s3_recv,
                 hsend, hrecv, osend, orecv):
    me = lax.axis_index("frame")
    z = me // LAYER
    inner = me % LAYER
    col = inner // CORES
    core = inner % CORES
    other = 1 - core
    yy = col // 2
    xx = col % 2

    def dev(layer, column, which):
        return {"frame": layer * LAYER + column * CORES + which}

    def near(o):
        return 2 * ((yy + o // 2) % 2) + (xx + o % 2) % 2

    sib = dev(z, col, other)

    def rcopy(src, dst, ssem, rsem, to):
        return pltpu.make_async_remote_copy(
            src_ref=src, dst_ref=dst, send_sem=ssem, recv_sem=rsem,
            device_id=to, device_id_type=pl.DeviceIdType.MESH)

    barrier = pltpu.get_barrier_semaphore()
    for step in range(1, LAYER):
        pl.semaphore_signal(barrier, inc=1, device_id={"frame": z * LAYER + (inner + step) % LAYER},
                            device_id_type=pl.DeviceIdType.MESH)
    for step in range(1, depth):
        for which in range(CORES):
            pl.semaphore_signal(barrier, inc=1, device_id=dev((z + step) % depth, col, which),
                                device_id_type=pl.DeviceIdType.MESH)
    pl.semaphore_wait(barrier, LAYER - 1 + (depth - 1) * CORES)

    to_col = inner % COLUMNS
    to_core = inner // COLUMNS
    keep = jnp.logical_and(to_col == col, to_core == core)

    def move():
        return rcopy(wkv_ref, wkvb.at[z, to_core], move_send.at[0], wrecv.at[z, 1, to_core], dev(z, to_col, to_core))

    kv_local = pltpu.make_async_copy(wkv_ref, wkvb.at[z, core], local_sem.at[1])
    q_local = pltpu.make_async_copy(wq_ref, wqb.at[z, core], local_sem.at[0])

    @pl.when(jnp.logical_not(keep))
    def _():
        move().start()

    @pl.when(keep)
    def _():
        kv_local.start()

    q_local.start()

    def wslot(t, part, c):
        return (wqb, wkvb)[part].at[t, c]

    def zcopy(t, part, way):
        src = wslot(t, part, core)
        return rcopy(src, src, zsend.at[(way + 1) // 2, t, part], wrecv.at[t, part, core], dev(z + way, col, core))

    def sibcopy(t, part):
        src = wslot(t, part, core)
        return rcopy(src, src, sibsend.at[t, part], wrecv.at[t, part, core], sib)

    def sends_of(t, part, way, act):
        @pl.when(jnp.logical_and(z + way >= 0, z + way < depth))
        def _():
            act(zcopy(t, part, way))

    def begin(c):
        c.start()

    def pass_on(k, part):
        for way in (1, -1):
            t = z - way * k

            @pl.when(jnp.logical_and(t >= 0, t < depth))
            def _():
                sibcopy(t, part).wait_recv()
                sends_of(t, part, way, begin)
                sibcopy(t, part).start()

    side = (None, dev(z, near(1), core), dev(z, near(2), core))

    def tcopy(o, h):
        return rcopy(tok_ref.at[h], tokbuf.at[col, h], tsend.at[o - 1, h], trecv.at[col, h], side[o])

    def tforward(o):
        b, h = near(o), o - 1
        return rcopy(tokbuf.at[b, h], tokbuf.at[b, h], tfsend.at[o - 1], trecv.at[b, h], side[3 - o])

    def twait(o, h):
        b = near(o)
        rcopy(tokbuf.at[b, h], tokbuf.at[b, h], tfsend.at[0], trecv.at[b, h], side[1]).wait_recv()

    q_local.wait()
    sends_of(z, 0, 1, begin)
    sends_of(z, 0, -1, begin)
    sibcopy(z, 0).start()

    def norm_into(b, halves):
        feat = nbuf.shape[1] // 2
        squares = 0.0
        for h in range(2):
            values = halves(h).astype(jnp.float32)
            squares = squares + jnp.sum(values * values, axis=0, keepdims=True)
        scale_inv = lax.rsqrt(squares / nbuf.shape[1] + epsilon)
        for h in range(2):
            nbuf[b, pl.ds(h * feat, feat)] = (halves(h).astype(jnp.float32) * scale_inv).astype(jnp.bfloat16)

    norm_into(col, lambda h: tok_ref[h])

    @pl.when(keep)
    def _():
        kv_local.wait()

    @pl.when(jnp.logical_not(keep))
    def _():
        rcopy(wkv_ref, wkvb.at[z, core], move_send.at[0], wrecv.at[z, 1, core], sib).wait_recv()

    sends_of(z, 1, 1, begin)
    sends_of(z, 1, -1, begin)
    sibcopy(z, 1).start()
    tcopy(1, 0).start()
    tcopy(2, 1).start()
    tcopy(1, 1).start()
    tcopy(2, 0).start()

    def sib_wait(k):
        for way in ((1, -1) if k else (1,)):
            t = z - way * k

            @pl.when(jnp.logical_and(t >= 0, t < depth))
            def _():
                for part in range(2):
                    slot = wslot(t, part, other)
                    rcopy(slot, slot, sibsend.at[t, part], wrecv.at[t, part, other], sib).wait_recv()

    def project(t, o):
        b = near(o)
        toks = nbuf[b]
        parts = [jnp.dot(wqb[t, c], toks, preferred_element_type=jnp.float32) for c in range(2)]
        kv = wkvb[t].reshape(2 * wkvb.shape[2], wkvb.shape[3])
        lin = jnp.dot(kv, toks, preferred_element_type=jnp.float32)
        query = jnp.concatenate(parts, axis=0)
        floor = jnp.where(t < depth // 2, 0.0, LOWEST)
        feats[t, b, 0] = jnp.maximum(query, 0.0).astype(jnp.bfloat16)
        lin = jnp.maximum(lin, floor).astype(jnp.bfloat16)
        feats[t, b, 1] = lin[:HDIM]
        feats[t, b, 2] = lin[HDIM:]

    def compute(count, offset_of, o_from, o_count):
        def body(i, carry):
            t = z + offset_of(i // o_count)

            @pl.when(jnp.logical_and(t >= 0, t < depth))
            def _():
                project(t, o_from + i % o_count)
            return carry
        lax.fori_loop(0, count * o_count, body, 0)

    def norm_recv(o):
        b = near(o)
        norm_into(b, lambda h: tokbuf[b, h])

    pass_on(1, 0)
    sib_wait(0)
    compute(1, lambda i: 0, 0, 1)
    pass_on(1, 1)
    twait(1, 0)
    tforward(1).start()
    twait(2, 1)
    tforward(2).start()
    sib_wait(1)
    compute(2, lambda i: 2 * i - 1, 0, 1)
    pass_on(2, 0)
    twait(1, 1)
    norm_recv(1)
    twait(2, 0)
    norm_recv(2)
    compute(3, lambda i: i - 1, 1, 2)
    pass_on(2, 1)
    sib_wait(2)
    compute(2, lambda i: 4 * i - 2, 0, 3)
    pass_on(3, 0)
    twait(3, 0)
    twait(3, 1)
    norm_recv(3)
    compute(5, lambda i: i - 2, 3, 1)
    pass_on(3, 1)
    sib_wait(3)
    compute(2, lambda i: 6 * i - 3, 0, 4)

    half = depth // 2
    ones = jnp.ones((st.shape[1] - HDIM, feats.shape[4]), jnp.bfloat16)
    for t in range(depth):
        total = None
        for b in range(COLUMNS):
            values = jnp.concatenate([feats[half + t // 2, b, 1 + t % 2], ones], axis=0)
            term = lax.dot_general(values, feats[t // 2, b, 1 + t % 2], NT, preferred_element_type=jnp.float32)
            total = term if total is None else total + term
        st[t] = total
    first = rcopy(st.at[pl.ds(2 * other, 2)], sib_in, s1_send.at[0], s1_recv.at[0], sib)
    first.start()
    first.wait()
    mine = (st[pl.ds(2 * core, 2)] + sib_in[...]).astype(jnp.bfloat16)
    st_out[...] = mine
    st_in[z] = mine

    def across(step):
        return rcopy(st_out, st_in.at[z], s2_send.at[step], s2_recv.at[z], dev((z + step) % depth, col, core))

    for step in range(1, depth):
        across(step).start()
    for step in range(1, depth):
        came = (z + step) % depth
        rcopy(st_out, st_in.at[came], s2_send.at[step], s2_recv.at[came], sib).wait_recv()
    total = st_in[0].astype(jnp.float32)
    for t in range(1, depth):
        total = total + st_in[t].astype(jnp.float32)
    st_sum[...] = total
    full[pl.ds(2 * core, 2)] = total
    third = rcopy(st_sum, full.at[pl.ds(2 * core, 2)], s3_send.at[0], s3_recv.at[0], sib)
    third.start()
    rcopy(st_sum, full.at[pl.ds(2 * other, 2)], s3_send.at[0], s3_recv.at[0], sib).wait_recv()

    def hcopy(way, t):
        d = (way + 1) // 2
        return rcopy(att.at[t, pl.ds(2 * d, 2)], halo.at[d, t], hsend.at[d, t], hrecv.at[d, t], dev(z + way, col, core))

    for way in (1, -1):
        @pl.when(jnp.logical_or(z - way < 0, z - way >= depth))
        def _():
            halo[(way + 1) // 2] = jnp.zeros(halo.shape[1:], halo.dtype)

    for t in range(depth):
        whole = full[t]
        high = whole.astype(jnp.bfloat16)
        low = (whole - high.astype(jnp.float32)).astype(jnp.bfloat16)
        for b in range(COLUMNS):
            query = feats[t, b, 0]
            both = (jnp.dot(high, query, preferred_element_type=jnp.float32)
                    + jnp.dot(low, query, preferred_element_type=jnp.float32))
            att[t, b] = (both[:HDIM] / (both[HDIM:HDIM + 1] + epsilon)).astype(jnp.bfloat16)
        for way in (1, -1):
            @pl.when(jnp.logical_and(z + way >= 0, z + way < depth))
            def _():
                hcopy(way, t).start()

    def ocopy(t, o):
        b = near(o)
        return rcopy(mixbuf.at[t, b], out_ref.at[t, col], osend.at[t, o], orecv.at[t, col], dev(z, b, core))

    turned = taps_ref[...].T

    for t in range(depth):
        for way in (1, -1):
            @pl.when(jnp.logical_and(z - way >= 0, z - way < depth))
            def _():
                hcopy(way, t).wait_recv()
        for x in range(2):
            even = att[t, x].astype(jnp.float32)
            odd = att[t, 2 + x].astype(jnp.float32)
            before = halo[1, t, x].astype(jnp.float32)
            after = halo[0, t, x].astype(jnp.float32)
            w = [turned[:HDIM, k * depth + t:k * depth + t + 1] for k in range(3)]
            mixbuf[t, x] = (w[0] * before + w[1] * even + w[2] * odd).astype(jnp.bfloat16)
            mixbuf[t, 2 + x] = (w[0] * even + w[1] * odd + w[2] * after).astype(jnp.bfloat16)
        for o in range(1, COLUMNS):
            ocopy(t, o).start()
        out_ref[t, col] = mixbuf[t, col]

    for t in range(depth):
        for o in range(1, COLUMNS):
            b = near(o)
            rcopy(mixbuf.at[t, b], out_ref.at[t, b], osend.at[t, o], orecv.at[t, b], dev(z, b, core)).wait_recv()
            ocopy(t, o).wait_send()
        for way in (1, -1):
            @pl.when(jnp.logical_and(z + way >= 0, z + way < depth))
            def _():
                hcopy(way, t).wait_send()
    third.wait_send()
    for step in range(1, depth):
        across(step).wait_send()

    @pl.when(jnp.logical_not(keep))
    def _():
        move().wait_send()

    for o in (1, 2):
        for h in range(2):
            tcopy(o, h).wait_send()
        tforward(o).wait_send()
    for t in range(depth):
        for part in range(2):
            sibcopy(t, part).wait_send()
            for way in (1, -1):
                @pl.when(way * (z - t) >= 0)
                def _():
                    sends_of(t, part, way, lambda c: c.wait_send())


def fused(tokens, w_query, w_keyval, taps):
    rows, width = tokens.shape
    depth = lax.axis_size("frame") // LAYER
    bf16, f32 = jnp.bfloat16, jnp.float32
    col = lax.axis_index("frame") % LAYER // CORES
    by_head = taps.reshape(taps.shape[0], HEADS // COLUMNS, COLUMNS, HDIM)
    own_taps = lax.dynamic_index_in_dim(by_head, col, 2, keepdims=False).reshape(-1, HDIM)
    own_taps = jnp.pad(own_taps, ((0, 128 - own_taps.shape[0]), (0, 128 - HDIM)))
    dma = lambda *s: pltpu.SemaphoreType.DMA(s)
    ext = HDIM + 16
    vmem = pl.BlockSpec(memory_space=pltpu.VMEM)
    out = pl.pallas_call(
        lambda *refs: fused_kernel(depth, *refs),
        out_shape=jax.ShapeDtypeStruct((depth, COLUMNS, HDIM, rows), bf16),
        in_specs=[vmem] * 4,
        out_specs=vmem,
        scratch_shapes=[
            pltpu.VMEM((COLUMNS, 2, width // 2, rows), bf16),
            pltpu.VMEM((COLUMNS, width, rows), bf16),
            pltpu.VMEM((depth, 2, w_query.shape[0], width), bf16),
            pltpu.VMEM((depth, 2, w_keyval.shape[0], width), bf16),
            pltpu.VMEM((depth, COLUMNS, 3, HDIM, rows), bf16),
            pltpu.VMEM((depth, ext, HDIM), f32),
            pltpu.VMEM((2, ext, HDIM), f32),
            pltpu.VMEM((2, ext, HDIM), bf16),
            pltpu.VMEM((depth, 2, ext, HDIM), bf16),
            pltpu.VMEM((2, ext, HDIM), f32),
            pltpu.VMEM((depth, ext, HDIM), f32),
            pltpu.VMEM((depth, COLUMNS, HDIM, rows), bf16),
            pltpu.VMEM((2, depth, 2, HDIM, rows), bf16),
            pltpu.VMEM((depth, COLUMNS, HDIM, rows), bf16),
            dma(2), dma(1), dma(depth, 2, 2), dma(2, depth, 2), dma(depth, 2),
            dma(COLUMNS, 2), dma(2, 2), dma(2),
            dma(1), dma(1), dma(depth), dma(depth), dma(1), dma(1),
            dma(2, depth), dma(2, depth), dma(depth, COLUMNS), dma(depth, COLUMNS),
        ],
        compiler_params=pltpu.CompilerParams(collective_id=0, has_side_effects=True, vmem_limit_bytes=60000 * 1024),
    )(tokens.T.reshape(2, width // 2, rows), w_query, w_keyval, own_taps)
    return out.reshape(HEADS * HDIM, rows).T


def fits(count, tokens, w_query, w_keyval):
    return (
        w_keyval.shape[0] // count == HDIM
        and 2 * w_query.shape[0] // count == HDIM
        and count % LAYER == 0
        and count // LAYER * COLUMNS == HEADS
        and HEIGHT * WIDTH // (tokens.shape[0] // count) == COLUMNS
    )


def solution(mesh):
    placed = (P(("grp", "frame"), None), P("frame", None), P("frame", None), P())

    def step(tokens, w_query, w_keyval, taps):
        groups, count = mesh.shape["grp"], mesh.shape["frame"]
        part = jax.ShapeDtypeStruct((tokens.shape[0] // groups,) + tokens.shape[1:], tokens.dtype)
        body = fused if fits(count, part, w_query, w_keyval) else local
        return jax.shard_map(
            body, mesh=mesh, in_specs=placed, out_specs=P(("grp", "frame"), None), check_vma=False
        )(tokens, w_query, w_keyval, taps)

    return step
```

```python
import jax
import jax.numpy as jnp
from jax import lax
from jax.experimental import pallas as pl
from jax.experimental.pallas import tpu as pltpu
from jax.sharding import PartitionSpec as P

HEADS = 16
HDIM = 112
HEIGHT = 32
WIDTH = 32


epsilon = 1e-06


def from_behind(value, axis, steps):
    count = lax.axis_size(axis)
    leading, last = (max(0, -steps), min(count, count - steps))
    return lax.ppermute(value, axis, [(source, source + steps) for source in range(leading, last)])


def normalize(rows_in):
    values = rows_in.astype(jnp.float32)
    scale_inv = lax.rsqrt(jnp.mean(values * values, axis=-1, keepdims=True) + epsilon)
    return (values * scale_inv).astype(jnp.bfloat16)


def local(tokens, w_query, w_keyval, taps):
    channels = HEADS * HDIM
    rows_here = tokens.shape[0]
    normed = normalize(tokens)

    def project_rows(weight_rows):
        return lax.dot_general(
            normed, weight_rows, (((1,), (1,)), ((), ())), preferred_element_type=jnp.float32
        )

    keyval_lin = project_rows(lax.all_gather(w_keyval, "frame", axis=0, tiled=True))
    key_feats = jax.nn.relu(keyval_lin[:, :channels]).astype(jnp.bfloat16)
    value_proj = keyval_lin[:, channels:].astype(jnp.bfloat16)
    key_heads = key_feats.reshape(rows_here, HEADS, HDIM)
    value_heads = value_proj.reshape(rows_here, HEADS, HDIM)
    local_state = jnp.einsum(
        "thd,the->hde", key_heads, value_heads, preferred_element_type=jnp.float32
    )
    local_keys = jnp.sum(key_heads.astype(jnp.float32), axis=0)
    query_lin = project_rows(lax.all_gather(w_query, "frame", axis=0, tiled=True))
    query_feats = jax.nn.relu(query_lin).astype(jnp.bfloat16)
    state, key_total = lax.psum((local_state, local_keys), "frame")
    query_heads = query_feats.reshape(rows_here, HEADS, HDIM).astype(jnp.float32)
    numer = jnp.einsum("thd,hde->the", query_heads, state, precision=lax.Precision.HIGHEST)
    denom = (
        jnp.einsum("thd,hd->th", query_heads, key_total, precision=lax.Precision.HIGHEST) + epsilon
    )
    attended = (numer / denom[:, :, None]).reshape(rows_here, channels).astype(jnp.bfloat16)
    strips = HEIGHT * WIDTH // rows_here
    earlier = from_behind(attended, "frame", strips)
    later_frame = from_behind(attended, "frame", -strips)
    mixed = (
        taps[0] * earlier.astype(jnp.float32)
        + taps[1] * attended.astype(jnp.float32)
        + taps[2] * later_frame.astype(jnp.float32)
    ).astype(jnp.bfloat16)
    return mixed


COLUMNS = 4
CORES = 2
LAYER = COLUMNS * CORES
LOWEST = -3.0e38
NT = (((1,), (1,)), ((), ()))


def fused_kernel(depth, tok_ref, wq_ref, wkv_ref, taps_ref, out_ref,
                 tokbuf, nbuf, wqb, wkvb, feats, st, sib_in, st_out, st_in, st_sum, full,
                 att, halo, mixbuf,
                 local_sem, move_send, wrecv, zsend, sibsend, trecv, tsend, tfsend,
                 s1_send, s1_recv, s2_send, s2_recv, s3_send, s3_recv,
                 hsend, hrecv, osend, orecv):
    me = lax.axis_index("frame")
    z = me // LAYER
    inner = me % LAYER
    col = inner // CORES
    core = inner % CORES
    other = 1 - core
    yy = col // 2
    xx = col % 2

    def dev(layer, column, which):
        return {"frame": layer * LAYER + column * CORES + which}

    def near(o):
        return 2 * ((yy + o // 2) % 2) + (xx + o % 2) % 2

    sib = dev(z, col, other)

    def rcopy(src, dst, ssem, rsem, to):
        return pltpu.make_async_remote_copy(
            src_ref=src, dst_ref=dst, send_sem=ssem, recv_sem=rsem,
            device_id=to, device_id_type=pl.DeviceIdType.MESH)

    barrier = pltpu.get_barrier_semaphore()
    for step in range(1, LAYER):
        pl.semaphore_signal(barrier, inc=1, device_id={"frame": z * LAYER + (inner + step) % LAYER},
                            device_id_type=pl.DeviceIdType.MESH)
    for step in range(1, depth):
        for which in range(CORES):
            pl.semaphore_signal(barrier, inc=1, device_id=dev((z + step) % depth, col, which),
                                device_id_type=pl.DeviceIdType.MESH)
    pl.semaphore_wait(barrier, LAYER - 1 + (depth - 1) * CORES)

    to_col = inner % COLUMNS
    to_core = inner // COLUMNS
    keep = jnp.logical_and(to_col == col, to_core == core)

    def move():
        return rcopy(wkv_ref, wkvb.at[z, to_core], move_send.at[0], wrecv.at[z, 1, to_core], dev(z, to_col, to_core))

    kv_local = pltpu.make_async_copy(wkv_ref, wkvb.at[z, core], local_sem.at[1])
    q_local = pltpu.make_async_copy(wq_ref, wqb.at[z, core], local_sem.at[0])

    @pl.when(jnp.logical_not(keep))
    def _():
        move().start()

    @pl.when(keep)
    def _():
        kv_local.start()

    q_local.start()

    def wslot(t, part, c):
        return (wqb, wkvb)[part].at[t, c]

    def zcopy(t, part, way):
        src = wslot(t, part, core)
        return rcopy(src, src, zsend.at[(way + 1) // 2, t, part], wrecv.at[t, part, core], dev(z + way, col, core))

    def sibcopy(t, part):
        src = wslot(t, part, core)
        return rcopy(src, src, sibsend.at[t, part], wrecv.at[t, part, core], sib)

    def sends_of(t, part, way, act):
        @pl.when(jnp.logical_and(z + way >= 0, z + way < depth))
        def _():
            act(zcopy(t, part, way))

    def begin(c):
        c.start()

    def pass_on(k, part):
        for way in (1, -1):
            t = z - way * k

            @pl.when(jnp.logical_and(t >= 0, t < depth))
            def _():
                sibcopy(t, part).wait_recv()
                sends_of(t, part, way, begin)
                sibcopy(t, part).start()

    side = (None, dev(z, near(1), core), dev(z, near(2), core))

    def tcopy(o, h):
        return rcopy(tok_ref.at[h], tokbuf.at[col, h], tsend.at[o - 1, h], trecv.at[col, h], side[o])

    def tforward(o):
        b, h = near(o), o - 1
        return rcopy(tokbuf.at[b, h], tokbuf.at[b, h], tfsend.at[o - 1], trecv.at[b, h], side[3 - o])

    def twait(o, h):
        b = near(o)
        rcopy(tokbuf.at[b, h], tokbuf.at[b, h], tfsend.at[0], trecv.at[b, h], side[1]).wait_recv()

    q_local.wait()
    sends_of(z, 0, 1, begin)
    sends_of(z, 0, -1, begin)
    sibcopy(z, 0).start()

    def norm_into(b, halves):
        feat = nbuf.shape[1] // 2
        squares = 0.0
        for h in range(2):
            values = halves(h).astype(jnp.float32)
            squares = squares + jnp.sum(values * values, axis=0, keepdims=True)
        scale_inv = lax.rsqrt(squares / nbuf.shape[1] + epsilon)
        for h in range(2):
            nbuf[b, pl.ds(h * feat, feat)] = (halves(h).astype(jnp.float32) * scale_inv).astype(jnp.bfloat16)

    norm_into(col, lambda h: tok_ref[h])

    pass_on(1, 0)

    @pl.when(keep)
    def _():
        kv_local.wait()

    @pl.when(jnp.logical_not(keep))
    def _():
        rcopy(wkv_ref, wkvb.at[z, core], move_send.at[0], wrecv.at[z, 1, core], sib).wait_recv()

    sends_of(z, 1, 1, begin)
    sends_of(z, 1, -1, begin)
    sibcopy(z, 1).start()
    tcopy(1, 0).start()
    tcopy(2, 1).start()
    tcopy(1, 1).start()
    tcopy(2, 0).start()

    def sib_wait(k):
        for way in ((1, -1) if k else (1,)):
            t = z - way * k

            @pl.when(jnp.logical_and(t >= 0, t < depth))
            def _():
                for part in range(2):
                    slot = wslot(t, part, other)
                    rcopy(slot, slot, sibsend.at[t, part], wrecv.at[t, part, other], sib).wait_recv()

    def project(t, o):
        b = near(o)
        toks = nbuf[b]
        parts = [jnp.dot(wqb[t, c], toks, preferred_element_type=jnp.float32) for c in range(2)]
        kv = wkvb[t].reshape(2 * wkvb.shape[2], wkvb.shape[3])
        lin = jnp.dot(kv, toks, preferred_element_type=jnp.float32)
        query = jnp.concatenate(parts, axis=0)
        floor = jnp.where(t < depth // 2, 0.0, LOWEST)
        feats[t, b, 0] = jnp.maximum(query, 0.0).astype(jnp.bfloat16)
        lin = jnp.maximum(lin, floor).astype(jnp.bfloat16)
        feats[t, b, 1] = lin[:HDIM]
        feats[t, b, 2] = lin[HDIM:]

    def compute(count, offset_of, o_from, o_count):
        def body(i, carry):
            t = z + offset_of(i // o_count)

            @pl.when(jnp.logical_and(t >= 0, t < depth))
            def _():
                project(t, o_from + i % o_count)
            return carry
        lax.fori_loop(0, count * o_count, body, 0)

    def norm_recv(o):
        b = near(o)
        norm_into(b, lambda h: tokbuf[b, h])

    pass_on(2, 0)
    sib_wait(0)
    compute(1, lambda i: 0, 0, 1)
    pass_on(3, 0)
    pass_on(1, 1)
    twait(1, 0)
    tforward(1).start()
    twait(2, 1)
    tforward(2).start()
    sib_wait(1)
    compute(2, lambda i: 2 * i - 1, 0, 1)
    pass_on(2, 1)
    twait(1, 1)
    norm_recv(1)
    twait(2, 0)
    norm_recv(2)
    compute(3, lambda i: i - 1, 1, 2)
    sib_wait(2)
    compute(2, lambda i: 4 * i - 2, 0, 3)
    twait(3, 0)
    twait(3, 1)
    norm_recv(3)
    compute(5, lambda i: i - 2, 3, 1)
    pass_on(3, 1)
    sib_wait(3)
    compute(2, lambda i: 6 * i - 3, 0, 4)

    half = depth // 2
    ones = jnp.ones((st.shape[1] - HDIM, feats.shape[4]), jnp.bfloat16)
    for t in range(depth):
        total = None
        for b in range(COLUMNS):
            values = jnp.concatenate([feats[half + t // 2, b, 1 + t % 2], ones], axis=0)
            term = lax.dot_general(values, feats[t // 2, b, 1 + t % 2], NT, preferred_element_type=jnp.float32)
            total = term if total is None else total + term
        st[t] = total
    first = rcopy(st.at[pl.ds(2 * other, 2)], sib_in, s1_send.at[0], s1_recv.at[0], sib)
    first.start()
    first.wait()
    mine = (st[pl.ds(2 * core, 2)] + sib_in[...]).astype(jnp.bfloat16)
    st_out[...] = mine
    st_in[z] = mine

    def across(step):
        return rcopy(st_out, st_in.at[z], s2_send.at[step], s2_recv.at[z], dev((z + step) % depth, col, core))

    for step in range(1, depth):
        across(step).start()
    for step in range(1, depth):
        came = (z + step) % depth
        rcopy(st_out, st_in.at[came], s2_send.at[step], s2_recv.at[came], sib).wait_recv()
    total = st_in[0].astype(jnp.float32)
    for t in range(1, depth):
        total = total + st_in[t].astype(jnp.float32)
    st_sum[...] = total
    full[pl.ds(2 * core, 2)] = total
    third = rcopy(st_sum, full.at[pl.ds(2 * core, 2)], s3_send.at[0], s3_recv.at[0], sib)
    third.start()
    rcopy(st_sum, full.at[pl.ds(2 * other, 2)], s3_send.at[0], s3_recv.at[0], sib).wait_recv()

    def hcopy(way, t):
        d = (way + 1) // 2
        return rcopy(att.at[t, pl.ds(2 * d, 2)], halo.at[d, t], hsend.at[d, t], hrecv.at[d, t], dev(z + way, col, core))

    for way in (1, -1):
        @pl.when(jnp.logical_or(z - way < 0, z - way >= depth))
        def _():
            halo[(way + 1) // 2] = jnp.zeros(halo.shape[1:], halo.dtype)

    for t in range(depth):
        whole = full[t]
        high = whole.astype(jnp.bfloat16)
        low = (whole - high.astype(jnp.float32)).astype(jnp.bfloat16)
        for b in range(COLUMNS):
            query = feats[t, b, 0]
            both = (jnp.dot(high, query, preferred_element_type=jnp.float32)
                    + jnp.dot(low, query, preferred_element_type=jnp.float32))
            att[t, b] = (both[:HDIM] / (both[HDIM:HDIM + 1] + epsilon)).astype(jnp.bfloat16)
        for way in (1, -1):
            @pl.when(jnp.logical_and(z + way >= 0, z + way < depth))
            def _():
                hcopy(way, t).start()

    def ocopy(t, o):
        b = near(o)
        return rcopy(mixbuf.at[t, b], out_ref.at[t, col], osend.at[t, o], orecv.at[t, col], dev(z, b, core))

    turned = taps_ref[...].T

    for t in range(depth):
        for way in (1, -1):
            @pl.when(jnp.logical_and(z - way >= 0, z - way < depth))
            def _():
                hcopy(way, t).wait_recv()
        for x in range(2):
            even = att[t, x].astype(jnp.float32)
            odd = att[t, 2 + x].astype(jnp.float32)
            before = halo[1, t, x].astype(jnp.float32)
            after = halo[0, t, x].astype(jnp.float32)
            w = [turned[:HDIM, k * depth + t:k * depth + t + 1] for k in range(3)]
            mixbuf[t, x] = (w[0] * before + w[1] * even + w[2] * odd).astype(jnp.bfloat16)
            mixbuf[t, 2 + x] = (w[0] * even + w[1] * odd + w[2] * after).astype(jnp.bfloat16)
        for o in range(1, COLUMNS):
            ocopy(t, o).start()
        out_ref[t, col] = mixbuf[t, col]

    for t in range(depth):
        for o in range(1, COLUMNS):
            b = near(o)
            rcopy(mixbuf.at[t, b], out_ref.at[t, b], osend.at[t, o], orecv.at[t, b], dev(z, b, core)).wait_recv()
            ocopy(t, o).wait_send()
        for way in (1, -1):
            @pl.when(jnp.logical_and(z + way >= 0, z + way < depth))
            def _():
                hcopy(way, t).wait_send()
    third.wait_send()
    for step in range(1, depth):
        across(step).wait_send()

    @pl.when(jnp.logical_not(keep))
    def _():
        move().wait_send()

    for o in (1, 2):
        for h in range(2):
            tcopy(o, h).wait_send()
        tforward(o).wait_send()
    for t in range(depth):
        for part in range(2):
            sibcopy(t, part).wait_send()
            for way in (1, -1):
                @pl.when(way * (z - t) >= 0)
                def _():
                    sends_of(t, part, way, lambda c: c.wait_send())


def fused(tokens, w_query, w_keyval, taps):
    rows, width = tokens.shape
    depth = lax.axis_size("frame") // LAYER
    bf16, f32 = jnp.bfloat16, jnp.float32
    col = lax.axis_index("frame") % LAYER // CORES
    by_head = taps.reshape(taps.shape[0], HEADS // COLUMNS, COLUMNS, HDIM)
    own_taps = lax.dynamic_index_in_dim(by_head, col, 2, keepdims=False).reshape(-1, HDIM)
    own_taps = jnp.pad(own_taps, ((0, 128 - own_taps.shape[0]), (0, 128 - HDIM)))
    dma = lambda *s: pltpu.SemaphoreType.DMA(s)
    ext = HDIM + 16
    vmem = pl.BlockSpec(memory_space=pltpu.VMEM)
    out = pl.pallas_call(
        lambda *refs: fused_kernel(depth, *refs),
        out_shape=jax.ShapeDtypeStruct((depth, COLUMNS, HDIM, rows), bf16),
        in_specs=[vmem] * 4,
        out_specs=vmem,
        scratch_shapes=[
            pltpu.VMEM((COLUMNS, 2, width // 2, rows), bf16),
            pltpu.VMEM((COLUMNS, width, rows), bf16),
            pltpu.VMEM((depth, 2, w_query.shape[0], width), bf16),
            pltpu.VMEM((depth, 2, w_keyval.shape[0], width), bf16),
            pltpu.VMEM((depth, COLUMNS, 3, HDIM, rows), bf16),
            pltpu.VMEM((depth, ext, HDIM), f32),
            pltpu.VMEM((2, ext, HDIM), f32),
            pltpu.VMEM((2, ext, HDIM), bf16),
            pltpu.VMEM((depth, 2, ext, HDIM), bf16),
            pltpu.VMEM((2, ext, HDIM), f32),
            pltpu.VMEM((depth, ext, HDIM), f32),
            pltpu.VMEM((depth, COLUMNS, HDIM, rows), bf16),
            pltpu.VMEM((2, depth, 2, HDIM, rows), bf16),
            pltpu.VMEM((depth, COLUMNS, HDIM, rows), bf16),
            dma(2), dma(1), dma(depth, 2, 2), dma(2, depth, 2), dma(depth, 2),
            dma(COLUMNS, 2), dma(2, 2), dma(2),
            dma(1), dma(1), dma(depth), dma(depth), dma(1), dma(1),
            dma(2, depth), dma(2, depth), dma(depth, COLUMNS), dma(depth, COLUMNS),
        ],
        compiler_params=pltpu.CompilerParams(collective_id=0, has_side_effects=True, vmem_limit_bytes=60000 * 1024),
    )(tokens.T.reshape(2, width // 2, rows), w_query, w_keyval, own_taps)
    return out.reshape(HEADS * HDIM, rows).T


def fits(count, tokens, w_query, w_keyval):
    return (
        w_keyval.shape[0] // count == HDIM
        and 2 * w_query.shape[0] // count == HDIM
        and count % LAYER == 0
        and count // LAYER * COLUMNS == HEADS
        and HEIGHT * WIDTH // (tokens.shape[0] // count) == COLUMNS
    )


def solution(mesh):
    placed = (P(("grp", "frame"), None), P("frame", None), P("frame", None), P())

    def step(tokens, w_query, w_keyval, taps):
        groups, count = mesh.shape["grp"], mesh.shape["frame"]
        part = jax.ShapeDtypeStruct((tokens.shape[0] // groups,) + tokens.shape[1:], tokens.dtype)
        body = fused if fits(count, part, w_query, w_keyval) else local
        return jax.shard_map(
            body, mesh=mesh, in_specs=placed, out_specs=P(("grp", "frame"), None), check_vma=False
        )(tokens, w_query, w_keyval, taps)

    return step
```

```python
import jax
import jax.numpy as jnp
from jax import lax
from jax.experimental import pallas as pl
from jax.experimental.pallas import tpu as pltpu
from jax.sharding import PartitionSpec as P

HEADS = 16
HDIM = 112
HEIGHT = 32
WIDTH = 32


epsilon = 1e-06


def from_behind(value, axis, steps):
    count = lax.axis_size(axis)
    leading, last = (max(0, -steps), min(count, count - steps))
    return lax.ppermute(value, axis, [(source, source + steps) for source in range(leading, last)])


def normalize(rows_in):
    values = rows_in.astype(jnp.float32)
    scale_inv = lax.rsqrt(jnp.mean(values * values, axis=-1, keepdims=True) + epsilon)
    return (values * scale_inv).astype(jnp.bfloat16)


def local(tokens, w_query, w_keyval, taps):
    channels = HEADS * HDIM
    rows_here = tokens.shape[0]
    normed = normalize(tokens)

    def project_rows(weight_rows):
        return lax.dot_general(
            normed, weight_rows, (((1,), (1,)), ((), ())), preferred_element_type=jnp.float32
        )

    keyval_lin = project_rows(lax.all_gather(w_keyval, "frame", axis=0, tiled=True))
    key_feats = jax.nn.relu(keyval_lin[:, :channels]).astype(jnp.bfloat16)
    value_proj = keyval_lin[:, channels:].astype(jnp.bfloat16)
    key_heads = key_feats.reshape(rows_here, HEADS, HDIM)
    value_heads = value_proj.reshape(rows_here, HEADS, HDIM)
    local_state = jnp.einsum(
        "thd,the->hde", key_heads, value_heads, preferred_element_type=jnp.float32
    )
    local_keys = jnp.sum(key_heads.astype(jnp.float32), axis=0)
    query_lin = project_rows(lax.all_gather(w_query, "frame", axis=0, tiled=True))
    query_feats = jax.nn.relu(query_lin).astype(jnp.bfloat16)
    state, key_total = lax.psum((local_state, local_keys), "frame")
    query_heads = query_feats.reshape(rows_here, HEADS, HDIM).astype(jnp.float32)
    numer = jnp.einsum("thd,hde->the", query_heads, state, precision=lax.Precision.HIGHEST)
    denom = (
        jnp.einsum("thd,hd->th", query_heads, key_total, precision=lax.Precision.HIGHEST) + epsilon
    )
    attended = (numer / denom[:, :, None]).reshape(rows_here, channels).astype(jnp.bfloat16)
    strips = HEIGHT * WIDTH // rows_here
    earlier = from_behind(attended, "frame", strips)
    later_frame = from_behind(attended, "frame", -strips)
    mixed = (
        taps[0] * earlier.astype(jnp.float32)
        + taps[1] * attended.astype(jnp.float32)
        + taps[2] * later_frame.astype(jnp.float32)
    ).astype(jnp.bfloat16)
    return mixed


COLUMNS = 4
CORES = 2
LAYER = COLUMNS * CORES
LOWEST = -3.0e38
NT = (((1,), (1,)), ((), ()))


def fused_kernel(depth, tok_ref, wq_ref, wkv_ref, taps_ref, out_ref,
                 tokbuf, nbuf, wqb, wkvb, feats, st, sib_in, st_out, st_in, st_sum, full,
                 att, halo, mixbuf,
                 local_sem, move_send, wrecv, zsend, sibsend, trecv, tsend, tfsend,
                 s1_send, s1_recv, s2_send, s2_recv, s3_send, s3_recv,
                 hsend, hrecv, osend, orecv):
    me = lax.axis_index("frame")
    z = me // LAYER
    inner = me % LAYER
    col = inner // CORES
    core = inner % CORES
    other = 1 - core
    yy = col // 2
    xx = col % 2

    def dev(layer, column, which):
        return {"frame": layer * LAYER + column * CORES + which}

    def near(o):
        return 2 * ((yy + o // 2) % 2) + (xx + o % 2) % 2

    sib = dev(z, col, other)

    def rcopy(src, dst, ssem, rsem, to):
        return pltpu.make_async_remote_copy(
            src_ref=src, dst_ref=dst, send_sem=ssem, recv_sem=rsem,
            device_id=to, device_id_type=pl.DeviceIdType.MESH)

    barrier = pltpu.get_barrier_semaphore()
    for step in range(1, LAYER):
        pl.semaphore_signal(barrier, inc=1, device_id={"frame": z * LAYER + (inner + step) % LAYER},
                            device_id_type=pl.DeviceIdType.MESH)
    for step in range(1, depth):
        for which in range(CORES):
            pl.semaphore_signal(barrier, inc=1, device_id=dev((z + step) % depth, col, which),
                                device_id_type=pl.DeviceIdType.MESH)
    pl.semaphore_wait(barrier, LAYER - 1 + (depth - 1) * CORES)

    to_col = inner % COLUMNS
    to_core = inner // COLUMNS
    keep = jnp.logical_and(to_col == col, to_core == core)

    def move():
        return rcopy(wkv_ref, wkvb.at[z, to_core], move_send.at[0], wrecv.at[z, 1, to_core], dev(z, to_col, to_core))

    kv_local = pltpu.make_async_copy(wkv_ref, wkvb.at[z, core], local_sem.at[1])
    q_local = pltpu.make_async_copy(wq_ref, wqb.at[z, core], local_sem.at[0])

    @pl.when(jnp.logical_not(keep))
    def _():
        move().start()

    @pl.when(keep)
    def _():
        kv_local.start()

    q_local.start()

    def wslot(t, part, c):
        return (wqb, wkvb)[part].at[t, c]

    def zcopy(t, part, way):
        src = wslot(t, part, core)
        return rcopy(src, src, zsend.at[(way + 1) // 2, t, part], wrecv.at[t, part, core], dev(z + way, col, core))

    def sibcopy(t, part):
        src = wslot(t, part, core)
        return rcopy(src, src, sibsend.at[t, part], wrecv.at[t, part, core], sib)

    def sends_of(t, part, way, act):
        @pl.when(jnp.logical_and(z + way >= 0, z + way < depth))
        def _():
            act(zcopy(t, part, way))

    def begin(c):
        c.start()

    def pass_on(k, part):
        for way in (1, -1):
            t = z - way * k

            @pl.when(jnp.logical_and(t >= 0, t < depth))
            def _():
                sibcopy(t, part).wait_recv()
                sends_of(t, part, way, begin)
                sibcopy(t, part).start()

    side = (None, dev(z, near(1), core), dev(z, near(2), core))

    def tcopy(o, h):
        return rcopy(tok_ref.at[h], tokbuf.at[col, h], tsend.at[o - 1, h], trecv.at[col, h], side[o])

    def tforward(o):
        b, h = near(o), o - 1
        return rcopy(tokbuf.at[b, h], tokbuf.at[b, h], tfsend.at[o - 1], trecv.at[b, h], side[3 - o])

    def twait(o, h):
        b = near(o)
        rcopy(tokbuf.at[b, h], tokbuf.at[b, h], tfsend.at[0], trecv.at[b, h], side[1]).wait_recv()

    q_local.wait()
    sends_of(z, 0, 1, begin)
    sends_of(z, 0, -1, begin)
    sibcopy(z, 0).start()

    def norm_into(b, halves):
        feat = nbuf.shape[1] // 2
        squares = 0.0
        for h in range(2):
            values = halves(h).astype(jnp.float32)
            squares = squares + jnp.sum(values * values, axis=0, keepdims=True)
        scale_inv = lax.rsqrt(squares / nbuf.shape[1] + epsilon)
        for h in range(2):
            nbuf[b, pl.ds(h * feat, feat)] = (halves(h).astype(jnp.float32) * scale_inv).astype(jnp.bfloat16)

    norm_into(col, lambda h: tok_ref[h])

    pass_on(1, 0)
    tcopy(1, 0).start()
    tcopy(2, 1).start()

    @pl.when(keep)
    def _():
        kv_local.wait()

    @pl.when(jnp.logical_not(keep))
    def _():
        rcopy(wkv_ref, wkvb.at[z, core], move_send.at[0], wrecv.at[z, 1, core], sib).wait_recv()

    sends_of(z, 1, 1, begin)
    sends_of(z, 1, -1, begin)
    sibcopy(z, 1).start()
    tcopy(1, 1).start()
    tcopy(2, 0).start()

    def sib_wait(k):
        for way in ((1, -1) if k else (1,)):
            t = z - way * k

            @pl.when(jnp.logical_and(t >= 0, t < depth))
            def _():
                for part in range(2):
                    slot = wslot(t, part, other)
                    rcopy(slot, slot, sibsend.at[t, part], wrecv.at[t, part, other], sib).wait_recv()

    def project(t, o):
        b = near(o)
        toks = nbuf[b]
        parts = [jnp.dot(wqb[t, c], toks, preferred_element_type=jnp.float32) for c in range(2)]
        kv = wkvb[t].reshape(2 * wkvb.shape[2], wkvb.shape[3])
        lin = jnp.dot(kv, toks, preferred_element_type=jnp.float32)
        query = jnp.concatenate(parts, axis=0)
        floor = jnp.where(t < depth // 2, 0.0, LOWEST)
        feats[t, b, 0] = jnp.maximum(query, 0.0).astype(jnp.bfloat16)
        lin = jnp.maximum(lin, floor).astype(jnp.bfloat16)
        feats[t, b, 1] = lin[:HDIM]
        feats[t, b, 2] = lin[HDIM:]

    def compute(count, offset_of, o_from, o_count):
        def body(i, carry):
            t = z + offset_of(i // o_count)

            @pl.when(jnp.logical_and(t >= 0, t < depth))
            def _():
                project(t, o_from + i % o_count)
            return carry
        lax.fori_loop(0, count * o_count, body, 0)

    def norm_recv(o):
        b = near(o)
        norm_into(b, lambda h: tokbuf[b, h])

    pass_on(2, 0)
    sib_wait(0)
    compute(1, lambda i: 0, 0, 1)
    pass_on(3, 0)
    pass_on(1, 1)
    twait(1, 0)
    tforward(1).start()
    twait(2, 1)
    tforward(2).start()
    sib_wait(1)
    compute(2, lambda i: 2 * i - 1, 0, 1)
    pass_on(2, 1)
    twait(1, 1)
    norm_recv(1)
    twait(2, 0)
    norm_recv(2)
    compute(3, lambda i: i - 1, 1, 2)
    sib_wait(2)
    compute(2, lambda i: 4 * i - 2, 0, 3)
    twait(3, 0)
    twait(3, 1)
    norm_recv(3)
    compute(5, lambda i: i - 2, 3, 1)
    pass_on(3, 1)
    sib_wait(3)
    compute(2, lambda i: 6 * i - 3, 0, 4)

    half = depth // 2
    ones = jnp.ones((st.shape[1] - HDIM, feats.shape[4]), jnp.bfloat16)
    for t in range(depth):
        total = None
        for b in range(COLUMNS):
            values = jnp.concatenate([feats[half + t // 2, b, 1 + t % 2], ones], axis=0)
            term = lax.dot_general(values, feats[t // 2, b, 1 + t % 2], NT, preferred_element_type=jnp.float32)
            total = term if total is None else total + term
        st[t] = total
    first = rcopy(st.at[pl.ds(2 * other, 2)], sib_in, s1_send.at[0], s1_recv.at[0], sib)
    first.start()
    first.wait()
    mine = (st[pl.ds(2 * core, 2)] + sib_in[...]).astype(jnp.bfloat16)
    st_out[...] = mine
    st_in[z] = mine

    def across(step):
        return rcopy(st_out, st_in.at[z], s2_send.at[step], s2_recv.at[z], dev((z + step) % depth, col, core))

    for step in range(1, depth):
        across(step).start()
    for step in range(1, depth):
        came = (z + step) % depth
        rcopy(st_out, st_in.at[came], s2_send.at[step], s2_recv.at[came], sib).wait_recv()
    total = st_in[0].astype(jnp.float32)
    for t in range(1, depth):
        total = total + st_in[t].astype(jnp.float32)
    st_sum[...] = total
    full[pl.ds(2 * core, 2)] = total
    third = rcopy(st_sum, full.at[pl.ds(2 * core, 2)], s3_send.at[0], s3_recv.at[0], sib)
    third.start()
    rcopy(st_sum, full.at[pl.ds(2 * other, 2)], s3_send.at[0], s3_recv.at[0], sib).wait_recv()

    def hcopy(way, t):
        d = (way + 1) // 2
        return rcopy(att.at[t, pl.ds(2 * d, 2)], halo.at[d, t], hsend.at[d, t], hrecv.at[d, t], dev(z + way, col, core))

    for way in (1, -1):
        @pl.when(jnp.logical_or(z - way < 0, z - way >= depth))
        def _():
            halo[(way + 1) // 2] = jnp.zeros(halo.shape[1:], halo.dtype)

    for t in range(depth):
        whole = full[t]
        high = whole.astype(jnp.bfloat16)
        low = (whole - high.astype(jnp.float32)).astype(jnp.bfloat16)
        for b in range(COLUMNS):
            query = feats[t, b, 0]
            both = (jnp.dot(high, query, preferred_element_type=jnp.float32)
                    + jnp.dot(low, query, preferred_element_type=jnp.float32))
            att[t, b] = (both[:HDIM] / (both[HDIM:HDIM + 1] + epsilon)).astype(jnp.bfloat16)
        for way in (1, -1):
            @pl.when(jnp.logical_and(z + way >= 0, z + way < depth))
            def _():
                hcopy(way, t).start()

    def ocopy(t, o):
        b = near(o)
        return rcopy(mixbuf.at[t, b], out_ref.at[t, col], osend.at[t, o], orecv.at[t, col], dev(z, b, core))

    turned = taps_ref[...].T

    for t in range(depth):
        for way in (1, -1):
            @pl.when(jnp.logical_and(z - way >= 0, z - way < depth))
            def _():
                hcopy(way, t).wait_recv()
        for x in range(2):
            even = att[t, x].astype(jnp.float32)
            odd = att[t, 2 + x].astype(jnp.float32)
            before = halo[1, t, x].astype(jnp.float32)
            after = halo[0, t, x].astype(jnp.float32)
            w = [turned[:HDIM, k * depth + t:k * depth + t + 1] for k in range(3)]
            mixbuf[t, x] = (w[0] * before + w[1] * even + w[2] * odd).astype(jnp.bfloat16)
            mixbuf[t, 2 + x] = (w[0] * even + w[1] * odd + w[2] * after).astype(jnp.bfloat16)
        for o in range(1, COLUMNS):
            ocopy(t, o).start()
        out_ref[t, col] = mixbuf[t, col]

    for t in range(depth):
        for o in range(1, COLUMNS):
            b = near(o)
            rcopy(mixbuf.at[t, b], out_ref.at[t, b], osend.at[t, o], orecv.at[t, b], dev(z, b, core)).wait_recv()
            ocopy(t, o).wait_send()
        for way in (1, -1):
            @pl.when(jnp.logical_and(z + way >= 0, z + way < depth))
            def _():
                hcopy(way, t).wait_send()
    third.wait_send()
    for step in range(1, depth):
        across(step).wait_send()

    @pl.when(jnp.logical_not(keep))
    def _():
        move().wait_send()

    for o in (1, 2):
        for h in range(2):
            tcopy(o, h).wait_send()
        tforward(o).wait_send()
    for t in range(depth):
        for part in range(2):
            sibcopy(t, part).wait_send()
            for way in (1, -1):
                @pl.when(way * (z - t) >= 0)
                def _():
                    sends_of(t, part, way, lambda c: c.wait_send())


def fused(tokens, w_query, w_keyval, taps):
    rows, width = tokens.shape
    depth = lax.axis_size("frame") // LAYER
    bf16, f32 = jnp.bfloat16, jnp.float32
    col = lax.axis_index("frame") % LAYER // CORES
    by_head = taps.reshape(taps.shape[0], HEADS // COLUMNS, COLUMNS, HDIM)
    own_taps = lax.dynamic_index_in_dim(by_head, col, 2, keepdims=False).reshape(-1, HDIM)
    own_taps = jnp.pad(own_taps, ((0, 128 - own_taps.shape[0]), (0, 128 - HDIM)))
    dma = lambda *s: pltpu.SemaphoreType.DMA(s)
    ext = HDIM + 16
    vmem = pl.BlockSpec(memory_space=pltpu.VMEM)
    out = pl.pallas_call(
        lambda *refs: fused_kernel(depth, *refs),
        out_shape=jax.ShapeDtypeStruct((depth, COLUMNS, HDIM, rows), bf16),
        in_specs=[vmem] * 4,
        out_specs=vmem,
        scratch_shapes=[
            pltpu.VMEM((COLUMNS, 2, width // 2, rows), bf16),
            pltpu.VMEM((COLUMNS, width, rows), bf16),
            pltpu.VMEM((depth, 2, w_query.shape[0], width), bf16),
            pltpu.VMEM((depth, 2, w_keyval.shape[0], width), bf16),
            pltpu.VMEM((depth, COLUMNS, 3, HDIM, rows), bf16),
            pltpu.VMEM((depth, ext, HDIM), f32),
            pltpu.VMEM((2, ext, HDIM), f32),
            pltpu.VMEM((2, ext, HDIM), bf16),
            pltpu.VMEM((depth, 2, ext, HDIM), bf16),
            pltpu.VMEM((2, ext, HDIM), f32),
            pltpu.VMEM((depth, ext, HDIM), f32),
            pltpu.VMEM((depth, COLUMNS, HDIM, rows), bf16),
            pltpu.VMEM((2, depth, 2, HDIM, rows), bf16),
            pltpu.VMEM((depth, COLUMNS, HDIM, rows), bf16),
            dma(2), dma(1), dma(depth, 2, 2), dma(2, depth, 2), dma(depth, 2),
            dma(COLUMNS, 2), dma(2, 2), dma(2),
            dma(1), dma(1), dma(depth), dma(depth), dma(1), dma(1),
            dma(2, depth), dma(2, depth), dma(depth, COLUMNS), dma(depth, COLUMNS),
        ],
        compiler_params=pltpu.CompilerParams(collective_id=0, has_side_effects=True, vmem_limit_bytes=60000 * 1024),
    )(tokens.T.reshape(2, width // 2, rows), w_query, w_keyval, own_taps)
    return out.reshape(HEADS * HDIM, rows).T


def fits(count, tokens, w_query, w_keyval):
    return (
        w_keyval.shape[0] // count == HDIM
        and 2 * w_query.shape[0] // count == HDIM
        and count % LAYER == 0
        and count // LAYER * COLUMNS == HEADS
        and HEIGHT * WIDTH // (tokens.shape[0] // count) == COLUMNS
    )


def solution(mesh):
    placed = (P(("grp", "frame"), None), P("frame", None), P("frame", None), P())

    def step(tokens, w_query, w_keyval, taps):
        groups, count = mesh.shape["grp"], mesh.shape["frame"]
        part = jax.ShapeDtypeStruct((tokens.shape[0] // groups,) + tokens.shape[1:], tokens.dtype)
        body = fused if fits(count, part, w_query, w_keyval) else local
        return jax.shard_map(
            body, mesh=mesh, in_specs=placed, out_specs=P(("grp", "frame"), None), check_vma=False
        )(tokens, w_query, w_keyval, taps)

    return step
```
